256 devices in a mesh: row: 16 (over z, x_hi), col: 16 (over y, x_lo, core).
Axes of the slice: x: 4 (x_hi: 2, x_lo: 2; x = x_hi * 2 + x_lo), y: 4, z: 8, core: 2. Of those that a mesh axis runs over, the one named last changes fastest.
Arguments:
- x_rhs: bfloat16 [32, 1024, 1024], P('col', 'row'), may hold values from -6 to 6
- panel_u: bfloat16 [32, 1024, 256], P('row', 'col'), may hold values from -0.1875 to 0.1875
- panel_v: bfloat16 [32, 1024, 256], P('row', 'col'), may hold values from -0.1875 to 0.1875
- panel_rank: int32 [32], replicated, may hold values from 32 to 256, as said below
- tile_p: bfloat16 [32, 32, 1024, 256], P('row', 'col'), may hold values from -0.0625 to 0.0625
- tile_q: bfloat16 [32, 32, 1024, 256], P('row', 'col'), may hold values from -0.1875 to 0.1875
- tile_rank: int32 [32, 32], P('row', 'col'), may hold values from 32 to 256, as said below
Outputs:
- kriged: bfloat16 [32, 1024, 1024], P('row', None, 'col')
The draws below stay inside these ranges and needn't reach their ends.
Inputs may be any that keep to these rules, and one draw needn't show every extreme that they name: `panel_rank`: each panel tile's rank; the columns at or beyond it carry no part of the tile. `tile_rank`: each trailing tile's rank; the columns at or beyond it carry no part of the tile.
All inputs are finite; a program needn't handle non-finite values.
Results may differ from the reference program's by a relative error of at most 0.018.
Values may be sent and summed in bfloat16 or wider, within the bound.
No kernel may reach another device: no remote copies, remote signals or barrier semaphores. Data moves between devices by JAX's collectives and lax.ppermute only.
A program may use at most 64 MiB of HBM per device.

```python
import jax
import jax.numpy as jnp
from jax import lax

B = 1024
R = 256
NRHS = 1024
NT = 32


def rank_values(key, shape):
    level_draw = jax.random.randint(jax.random.fold_in(key, 11), shape, 0, 16)
    low_rank = R // 8
    flat_ranks = (low_rank + level_draw * level_draw * (R - low_rank) // 225).reshape(-1)
    flat_ranks = jnp.minimum(flat_ranks, R).astype(jnp.int32)
    count_all = flat_ranks.shape[0]
    top_spot = jax.random.randint(jax.random.fold_in(key, 12), (), 0, count_all)
    step_away = jax.random.randint(jax.random.fold_in(key, 13), (), 1, count_all)
    bottom_spot = (top_spot + step_away) % count_all
    flat_ranks = flat_ranks.at[top_spot].set(R)
    flat_ranks = flat_ranks.at[bottom_spot].set(low_rank)
    return flat_ranks.reshape(shape).astype(jnp.int32)


def draw_panel_rank(key, part):
    return rank_values(jax.random.fold_in(key, 101), (NT,))


def draw_tile_rank(key, part):
    return rank_values(jax.random.fold_in(key, 202), (NT, NT))


def level_of(stream_key, extent, pieces, smallest, high):
    loudness = 1.0
    for position, shards_of in pieces:
        steps = jax.random.uniform(jax.random.fold_in(jax.random.fold_in(stream_key, 6), position), (shards_of,), jnp.float32, smallest / len(pieces), high / len(pieces))
        loudness = loudness * jnp.repeat(jnp.exp(steps), extent[position] // shards_of).reshape((-1,) + (1,) * (len(extent) - 1 - position))
    return loudness


def normal_values(own_key, shape, deviation, reach, shards=(), kind=jnp.bfloat16):
    array = jax.random.normal(own_key, shape, jnp.float32) * deviation
    if len(shards) > 0:
        array = level_of(own_key, shape, shards, -0.22, 0.18) * array
    return jnp.clip(array, min=-reach, max=reach).astype(kind)


def setup_inputs(seed: int = 0) -> dict:
    keys = jax.random.split(jax.random.key(seed), 8)
    return {
        "x_rhs": normal_values(keys[0], (NT, B, NRHS), 1.0, 6.0, ((0, 16), (1, 16))),
        "panel_u": normal_values(keys[1], (NT, B, R), B ** -0.5, 0.1875, ((0, 16), (1, 16))),
        "panel_v": normal_values(keys[2], (NT, B, R), (4 * R) ** -0.5, 0.1875, ((0, 16), (1, 16))),
        "panel_rank": draw_panel_rank(jax.random.fold_in(keys[7], 71), 0),
        "tile_p": normal_values(keys[4], (NT, NT, B, R), (R * NT) ** -0.5, 0.0625, ((0, 16), (1, 16))),
        "tile_q": normal_values(keys[5], (NT, NT, B, R), B ** -0.5, 0.1875, ((0, 16), (1, 16))),
        "tile_rank": draw_tile_rank(jax.random.fold_in(keys[7], 71), 0),
    }


def reference(x_rhs, panel_u, panel_v, panel_rank, tile_p, tile_q, tile_rank):
    exact = lax.Precision.HIGHEST
    rank_slot = jnp.arange(R, dtype=jnp.int32)
    rhs_wide = x_rhs.astype(jnp.float32)
    u_wide = panel_u.astype(jnp.float32)
    v_wide = panel_v.astype(jnp.float32)
    panel_mask = rank_slot[None, :, None] < panel_rank[:, None, None]
    panel_proj = jnp.einsum("jbr,jbn->jrn", u_wide, rhs_wide, precision=exact)
    panel_proj = jnp.where(panel_mask, panel_proj, jnp.float32(0.0)).astype(jnp.bfloat16)
    sweep = jnp.einsum("jbr,jrn->bn", v_wide, panel_proj.astype(jnp.float32), precision=exact)
    back_proj = jnp.einsum("ibr,bn->irn", v_wide, sweep, precision=exact)
    back_proj = jnp.where(panel_mask, back_proj, jnp.float32(0.0))
    correction = jnp.einsum("ibr,irn->ibn", u_wide, back_proj, precision=exact)

    def one_row(packed):
        p_row, q_row, rank_row = packed
        tile_proj = jnp.einsum("jbr,jbn->jrn", q_row.astype(jnp.float32), rhs_wide, precision=exact)
        tile_mask = rank_slot[None, :, None] < rank_row[:, None, None]
        tile_proj = jnp.where(tile_mask, tile_proj, jnp.float32(0.0)).astype(jnp.bfloat16)
        return jnp.einsum("jbr,jrn->bn", p_row.astype(jnp.float32), tile_proj.astype(jnp.float32), precision=exact)

    base_sum = lax.map(one_row, (tile_p, tile_q, tile_rank))
    return (base_sum - correction).astype(jnp.bfloat16)
```

```python
import functools

import jax
import jax.numpy as jnp
from jax import lax
from jax.experimental import pallas as pl
from jax.experimental.pallas import tpu as pltpu
from jax.sharding import Mesh
from jax.sharding import PartitionSpec as P

ALL = ("z", "xh", "y", "xl", "co")
ROW = ("z", "xh")
COL = ("y", "xl", "co")
BF = jnp.bfloat16
F32 = jnp.float32
ANY = pl.BlockSpec(memory_space=pl.ANY)
SMEM = pl.BlockSpec(memory_space=pltpu.SMEM)
VMEM = pl.BlockSpec(memory_space=pltpu.VMEM)


def shift(axis, k):
    n = lax.axis_size(axis)
    return [(i, (i + k) % n) for i in range(n)]


def move(a, axis, k):
    return lax.ppermute(a, axis, shift(axis, k))


def swap(a, axis, k=1):
    n = lax.axis_size(axis)
    return lax.ppermute(a, axis, [(i, i ^ k) for i in range(n)])


def split_kernel(at, x_ref, mine_ref, theirs_ref):
    first = at[4] == 0
    for y in range(4):
        a = x_ref[:, :, 256 * y : 256 * y + 128]
        b = x_ref[:, :, 256 * y + 128 : 256 * y + 256]
        low = jnp.concatenate([a[..., :64], b[..., :64]], axis=-1)
        high = jnp.concatenate([a[..., 64:], b[..., 64:]], axis=-1)
        mine_ref[:, :, 128 * y : 128 * y + 128] = jnp.where(first, low, high)
        theirs_ref[:, :, 128 * y : 128 * y + 128] = jnp.where(first, high, low)


def split_columns(at, x):
    half = jax.ShapeDtypeStruct((2, 64, 512), BF)
    return pl.pallas_call(
        split_kernel,
        out_shape=(half, half),
        in_specs=[SMEM, VMEM],
        out_specs=(VMEM, VMEM),
        compiler_params=pltpu.CompilerParams(vmem_limit_bytes=8 << 20),
        name="split_columns",
    )(at, x)


def fetch_x(at, pieces, x_s, sem, group=None):
    z, xh = at[0], at[1]
    copies = []
    for k, (ref, step, halves) in enumerate(pieces):
        for n, h in enumerate(halves):
            rows = lax.rem(z + step + 8, 8) * 128 + (xh if h == 0 else 1 - xh) * 64
            rows = pl.multiple_of(rows, 64)
            src = ref.at[n] if group is None else ref.at[n, group]
            dst = x_s.at[:, :, pl.ds(rows, 64), :] if group is None else x_s.at[:, pl.ds(rows, 64), :]
            copies.append(pltpu.make_async_copy(src, dst, sem))
    for c in copies:
        c.start()
    return copies


STEPS = ((0, (0, 1)), (-1, (0, 1)), (1, (0, 1)), (-2, (0, 1)), (2, (0, 1)), (-3, (0, 1)), (3, (0, 1)), (4, (0,)), (4, (1,)))


def proj_kernel(at, rank, *refs):
    pieces = [(r, s, h) for r, (s, h) in zip(refs[:9], STEPS, strict=True)]
    u_ref, out_ref, x_s, sem = refs[9:]
    group = jnp.where(at[4] == at[1], 0, 1)
    copies = fetch_x(at, pieces, x_s, sem, group)
    for c in copies:
        c.wait()
    slot = lax.broadcasted_iota(jnp.int32, (256, 1), 0)
    both = []
    for j in range(2):
        p = lax.dot_general(u_ref[j], x_s[j], (((0,), (0,)), ((), ())), preferred_element_type=F32)
        p = jnp.where(slot < rank[2 * (2 * at[0] + at[1]) + j], p, 0.0)
        both.append(p)
    for y in range(4):
        a, b = (p[:, 128 * y : 128 * y + 128] for p in both)
        out_ref[0, y] = jnp.concatenate([a[:, :64], b[:, :64]], axis=-1).astype(BF)
        out_ref[1, y] = jnp.concatenate([a[:, 64:], b[:, 64:]], axis=-1).astype(BF)


def project(at, panel_rank, pieces, u):
    return pl.pallas_call(
        proj_kernel,
        out_shape=jax.ShapeDtypeStruct((2, 4, 256, 128), BF),
        in_specs=[SMEM, SMEM] + [ANY] * 9 + [VMEM],
        out_specs=VMEM,
        scratch_shapes=[pltpu.VMEM((2, 1024, 512), BF), pltpu.SemaphoreType.DMA(())],
        compiler_params=pltpu.CompilerParams(vmem_limit_bytes=16 << 20),
        cost_estimate=pl.CostEstimate(flops=2 * 2 * 256 * 1024 * 512, bytes_accessed=4 << 20, transcendentals=0),
        name="project",
    )(at, panel_rank, *pieces, u)


def part_kernel(p_ref, v_ref, out_ref):
    lane = lax.broadcasted_iota(jnp.int32, (1, 128), 1)
    p = p_ref[...]
    zero = jnp.zeros_like(p)
    s = jnp.dot(v_ref[0], jnp.where(lane < 64, p, zero), preferred_element_type=F32)
    s += jnp.dot(v_ref[1], jnp.where(lane < 64, zero, p), preferred_element_type=F32)
    s += jnp.concatenate([s[:, 64:], s[:, :64]], axis=-1)
    out_ref[...] = jnp.where(lane < 64, s[:512], s[512:]).astype(BF)


def sweep_part(p, v):
    return pl.pallas_call(
        part_kernel,
        out_shape=jax.ShapeDtypeStruct((512, 128), BF),
        in_specs=[VMEM, VMEM],
        out_specs=VMEM,
        compiler_params=pltpu.CompilerParams(vmem_limit_bytes=8 << 20),
        cost_estimate=pl.CostEstimate(flops=2 * 2 * 256 * 1024 * 128, bytes_accessed=2 << 20, transcendentals=0),
        name="sweep_part",
    )(p, v)


def late_kernel(at, rank, s_ref, u_ref, v_ref, out_ref):
    lane = lax.broadcasted_iota(jnp.int32, (1, 128), 1)
    slot = lax.broadcasted_iota(jnp.int32, (256, 1), 0)
    packed = s_ref[...].astype(F32)
    turned = jnp.concatenate([packed[:, 64:], packed[:, :64]], axis=-1)
    s = jnp.concatenate([jnp.where(lane < 64, packed, turned), jnp.where(lane < 64, turned, packed)], axis=0)
    high = s.astype(BF)
    total = None
    for i in range(2):
        back = lax.dot_general(v_ref[i], high, (((0,), (0,)), ((), ())), preferred_element_type=F32)
        keep = jnp.logical_and(slot < rank[2 * (2 * at[0] + at[1]) + i], (lane < 64) == (i == 0))
        back = jnp.where(keep, back, 0.0).astype(BF)
        t = jnp.dot(u_ref[i], back, preferred_element_type=F32)
        total = t if total is None else total + t
    out_ref[...] = total


def late(at, panel_rank, s, u, v):
    return pl.pallas_call(
        late_kernel,
        out_shape=jax.ShapeDtypeStruct((1024, 128), F32),
        in_specs=[SMEM, SMEM, VMEM, VMEM, VMEM],
        out_specs=VMEM,
        compiler_params=pltpu.CompilerParams(vmem_limit_bytes=12 << 20),
        cost_estimate=pl.CostEstimate(flops=4 * 2 * 256 * 1024 * 128, bytes_accessed=3 << 20, transcendentals=0),
        name="late",
    )(at, panel_rank, s, u, v)


def base_kernel(at, rank_a, rank_b, *refs):
    pieces = [(r, s, h) for r, (s, h) in zip(refs[:9], STEPS, strict=True)]
    qa, qb, pa, pb = refs[9:13]
    plus_ref, minus_ref, own_ref, next_ref, prev_ref = refs[13:18]
    x_s, acc, sem = refs[18:]
    i, j = pl.program_id(0), pl.program_id(1)

    @pl.when(jnp.logical_and(i == 0, j == 0))
    def _():
        for c in fetch_x(at, pieces, x_s, sem):
            c.wait()

    slot = lax.broadcasted_iota(jnp.int32, (256, 1), 0)

    def term(q_ref, p_ref, rank, g, b):
        t = lax.dot_general(q_ref[0, 0], x_s[g, b], (((0,), (0,)), ((), ())), preferred_element_type=F32)
        t = jnp.where(slot < rank[i, b], t, 0.0).astype(BF)
        return jnp.dot(p_ref[0, 0], t, preferred_element_type=F32)

    @pl.when(j == 0)
    def _():
        acc[i] = term(qa, pa, rank_a, 0, 0)

    @pl.when(j == 1)
    def _():
        acc[i] += term(qa, pa, rank_a, 0, 1)

    @pl.when(j == 2)
    def _():
        acc[i] += term(qb, pb, rank_b, 1, 0)

    @pl.when(j == 3)
    def _():
        acc[i] += term(qb, pb, rank_b, 1, 1)

    @pl.when(jnp.logical_and(i == 1, j == 3))
    def _():
        def block(n, d):
            lanes = pl.multiple_of(lax.rem(at[2] + d, 4) * 128, 128)
            return acc[n, :, pl.ds(lanes, 128)]

        plus_ref[0] = block(0, 2).astype(BF)
        plus_ref[1] = block(1, 1).astype(BF)
        minus_ref[0] = block(1, 2).astype(BF)
        minus_ref[1] = block(0, 3).astype(BF)
        own_ref[0] = block(0, 0)
        own_ref[1] = block(1, 0)
        next_ref[...] = block(0, 1)
        prev_ref[...] = block(1, 3)


def base(at, rank_a, rank_b, pieces, qa, qb, pa, pb):
    first = pl.BlockSpec((1, 1, 1024, 256), lambda i, j: (i, jnp.minimum(j, 1), 0, 0))
    second = pl.BlockSpec((1, 1, 1024, 256), lambda i, j: (i, jnp.maximum(j - 2, 0), 0, 0))
    whole = lambda *s: pl.BlockSpec(s, lambda i, j: (0,) * len(s))
    return pl.pallas_call(
        base_kernel,
        grid=(2, 4),
        out_shape=(
            jax.ShapeDtypeStruct((2, 1024, 128), BF),
            jax.ShapeDtypeStruct((2, 1024, 128), BF),
            jax.ShapeDtypeStruct((2, 1024, 128), F32),
            jax.ShapeDtypeStruct((1024, 128), F32),
            jax.ShapeDtypeStruct((1024, 128), F32),
        ),
        in_specs=[SMEM, SMEM, SMEM] + [ANY] * 9 + [first, second, first, second],
        out_specs=(whole(2, 1024, 128), whole(2, 1024, 128), whole(2, 1024, 128), whole(1024, 128), whole(1024, 128)),
        scratch_shapes=[
            pltpu.VMEM((2, 2, 1024, 512), BF),
            pltpu.VMEM((2, 1024, 512), F32),
            pltpu.SemaphoreType.DMA(()),
        ],
        compiler_params=pltpu.CompilerParams(vmem_limit_bytes=40 << 20),
        cost_estimate=pl.CostEstimate(flops=8 * 2 * 2 * 256 * 1024 * 512, bytes_accessed=14 << 20, transcendentals=0),
        name="base",
    )(at, rank_a, rank_b, *pieces, qa, qb, pa, pb)


def pack_kernel(at, own_ref, plus_ref, minus_ref, low_ref, high_ref, keep_ref, send_ref):
    lane = lax.broadcasted_iota(jnp.int32, (1, 128), 1)
    a = own_ref[0] + minus_ref[1].astype(F32) + low_ref[...].astype(F32)
    b = own_ref[1] + plus_ref[1].astype(F32) + high_ref[...].astype(F32)
    turn = lambda v: jnp.concatenate([v[:, 64:], v[:, :64]], axis=-1)
    low = jnp.where(lane < 64, a, turn(b))
    high = jnp.where(lane < 64, turn(a), b)
    first = at[3] == 0
    keep_ref[...] = jnp.where(first, low, high)
    send_ref[...] = jnp.where(first, high, low).astype(BF)


def pack(at, own, plus, minus, low, high):
    return pl.pallas_call(
        pack_kernel,
        out_shape=(jax.ShapeDtypeStruct((1024, 128), F32), jax.ShapeDtypeStruct((1024, 128), BF)),
        in_specs=[SMEM] + [VMEM] * 5,
        out_specs=(VMEM, VMEM),
        compiler_params=pltpu.CompilerParams(vmem_limit_bytes=12 << 20),
        name="pack",
    )(at, own, plus, minus, low, high)


def last_kernel(keep_ref, came_ref, late_ref, out_ref):
    v = keep_ref[...] + came_ref[...].astype(F32) - late_ref[...]
    t = v.T.astype(BF)
    out_ref[0] = t[:64]
    out_ref[1] = t[64:]


def last(keep, came, correction):
    return pl.pallas_call(
        last_kernel,
        out_shape=jax.ShapeDtypeStruct((2, 64, 1024), BF),
        in_specs=[VMEM] * 3,
        out_specs=VMEM,
        compiler_params=pltpu.CompilerParams(vmem_limit_bytes=8 << 20),
        name="last",
    )(keep, came, correction)


def whole_panel(u, v):
    both = jnp.stack([u, v])
    other = swap(both, "xl")
    xl = lax.axis_index("xl")
    co = lax.axis_index("co")
    first = jnp.where(xl == 0, both, other)
    second = jnp.where(xl == 0, other, both)
    pair = jnp.stack([first, second])
    fp = move(pair, "y", 1)
    fm = move(pair, "y", -1)
    far = move(fp, "y", 1)
    y = lax.axis_index("y")
    four = jnp.stack([pair, fm, far, fp])
    mate = swap(four, "co")
    a = jnp.where(co == 0, four, mate)
    b = jnp.where(co == 0, mate, four)
    rows = jnp.stack([a, b], axis=2)
    rows = jnp.roll(rows, y, axis=0)
    rows = rows.transpose(3, 4, 0, 1, 2, 5, 6).reshape(2, 2, 1024, 256)
    return rows[0], rows[1]


def plane_pairs(axis_pairs):
    return axis_pairs


def shards(x_rhs, panel_u, panel_v, panel_rank, tile_p, tile_q, tile_rank):
    z, xh, y, xl, co = (lax.axis_index(a) for a in ALL)
    at = jnp.stack([z, xh, y, xl, co]).astype(jnp.int32)

    mine, theirs = split_columns(at, x_rhs)
    own = jnp.stack([mine, swap(theirs, "co")])
    piece = jnp.stack([own, swap(own, "xh")])
    qb = swap(tile_q, "co")
    pb = swap(tile_p, "co")
    rank_b = swap(tile_rank, "co")
    u, v = whole_panel(panel_u, panel_v)

    fp1, fm1 = move(piece, "z", 1), move(piece, "z", -1)
    fp2, fm2 = move(fp1, "z", 1), move(fm1, "z", -1)
    fp3, fm3 = move(fp2, "z", 1), move(fm2, "z", -1)
    fp4, fm4 = move(fp3[:1], "z", 1), move(fm3[1:], "z", -1)
    pieces = (piece, fp1, fm1, fp2, fm2, fp3, fm3, fp4, fm4)

    proj = project(at, panel_rank, pieces, u)
    n_z, n_h, n_y, n_l, n_c = (lax.axis_size(a) for a in ALL)

    def device(a, b, c, d, e):
        return (((a * n_h + b) * n_y + c) * n_l + d) * n_c + e

    spread = [(a, b, e) for a in range(n_z) for b in range(n_h) for e in range(n_c)]
    across = [(device(a, b, a >> 1, a & 1, e), device(a, b, a >> 1, 1 - (a & 1), e)) for a, b, e in spread]
    came = lax.ppermute(lax.dynamic_index_in_dim(proj, 1 - xl, 0, False), ALL, across)
    here = lax.dynamic_index_in_dim(proj, xl, 0, False)
    row = jnp.where(xl == lax.rem(z, 2), here, came)
    got = lax.dynamic_index_in_dim(row, y, 0, False)
    got = jnp.where(y == z // 2, got, jnp.zeros_like(got))
    for d in range(1, 4):
        along = [
            (device(a, b, a >> 1, f, e), device(a, b, ((a >> 1) + d) % 4, f, e)) for a, b, e in spread for f in range(n_l)
        ]
        got = got + lax.ppermute(lax.dynamic_index_in_dim(row, lax.rem(y + d, 4), 0, False), ALL, along)
    s = sweep_part(got, v)
    for axis, k in (("xh", 1), ("z", 1), ("z", 2), ("z", 4)):
        s = s + swap(s, axis, k)
    correction = late(at, panel_rank, s, u, v)

    plus, minus, own_sum, after, before = base(at, tile_rank, rank_b, pieces, tile_q, qb, tile_p, pb)
    plus, minus = move(plus, "y", 1), move(minus, "y", -1)
    low = move((after + plus[0].astype(F32)).astype(BF), "y", 1)
    high = move((before + minus[0].astype(F32)).astype(BF), "y", -1)
    keep, send = pack(at, own_sum, plus, minus, low, high)
    out = last(keep, swap(send, "xl"), correction)
    return out.swapaxes(1, 2)


def solution(mesh):
    finer = Mesh(mesh.devices.reshape(8, 2, 4, 2, 2), ALL)
    return jax.shard_map(
        shards,
        mesh=finer,
        in_specs=(
            P(COL, ROW, None),
            P(ROW, COL, None),
            P(ROW, COL, None),
            P(),
            P(ROW, COL, None, None),
            P(ROW, COL, None, None),
            P(ROW, COL),
        ),
        out_specs=P(ROW, None, COL),
        check_vma=False,
    )
```

```python
import jax
import jax.numpy as jnp
from jax import lax
from jax.experimental import pallas as pl
from jax.experimental.pallas import tpu as pltpu
from jax.sharding import Mesh
from jax.sharding import PartitionSpec as P

ALL = ("z", "xh", "y", "xl", "co")
ROW = ("z", "xh")
COL = ("y", "xl", "co")
BF = jnp.bfloat16
F32 = jnp.float32
ANY = pl.BlockSpec(memory_space=pl.ANY)
SMEM = pl.BlockSpec(memory_space=pltpu.SMEM)
VMEM = pl.BlockSpec(memory_space=pltpu.VMEM)


def move(a, axis, k):
    n = lax.axis_size(axis)
    return lax.ppermute(a, axis, [(i, (i + k) % n) for i in range(n)])


def swap(a, axis, k=1):
    n = lax.axis_size(axis)
    return lax.ppermute(a, axis, [(i, i ^ k) for i in range(n)])


def split_kernel(at, x_ref, mine_ref, theirs_ref):
    first = at[4] == 0
    for y in range(4):
        a = x_ref[:, :, 256 * y : 256 * y + 128]
        b = x_ref[:, :, 256 * y + 128 : 256 * y + 256]
        low = jnp.concatenate([a[..., :64], b[..., :64]], axis=-1)
        high = jnp.concatenate([a[..., 64:], b[..., 64:]], axis=-1)
        mine_ref[:, :, 128 * y : 128 * y + 128] = jnp.where(first, low, high)
        theirs_ref[:, :, 128 * y : 128 * y + 128] = jnp.where(first, high, low)


def split_columns(at, x):
    half = jax.ShapeDtypeStruct((2, 64, 512), BF)
    return pl.pallas_call(
        split_kernel,
        out_shape=(half, half),
        in_specs=[SMEM, VMEM],
        out_specs=(VMEM, VMEM),
        compiler_params=pltpu.CompilerParams(vmem_limit_bytes=8 << 20),
        name="split_columns",
    )(at, x)


EARLY = (
    (0, ((0, 0), (2, 1))),
    (-1, ((0, 0), (2, 1))),
    (1, ((0, 0), (2, 1))),
    (-2, ((0, 0), (2, 1))),
    (2, ((0, 0), (2, 1))),
    (-3, ((0, 0), (2, 1))),
    (3, ((0, 0), (2, 1))),
    (4, ((0, 0),)),
    (4, ((0, 1),)),
)
LATER = (
    (0, ((1, 0),)),
    (-1, ((1, 0),)),
    (1, ((1, 0),)),
    (-2, ((1, 0),)),
    (2, ((1, 0),)),
    (-3, ((1, 0),)),
    (3, ((1, 0),)),
    (4, ((1, 0),)),
)
CROSS = (((0, 0), (1, -1), (2, 1)), ((0, -2), (1, 2)), ((0, -3), (1, 3)), ((0, 4),))


def row_of(at, step, other):
    rows = lax.rem(at[0] + step + 8, 8) * 128 + (1 - at[1] if other else at[1]) * 64
    return pl.multiple_of(rows, 64)


def copies_early(at, refs, x_s, sem):
    return [
        pltpu.make_async_copy(ref.at[n], x_s.at[:, pl.ds(row_of(at, step, other), 64), :], sem)
        for ref, (step, blocks) in zip(refs, EARLY)
        for n, other in blocks
    ]


def copies_later(at, refs, crossed, x_s, sem):
    found = [
        pltpu.make_async_copy(ref.at[n], x_s.at[:, pl.ds(row_of(at, step, other), 64), :], sem)
        for ref, (step, blocks) in zip(refs, LATER, strict=True)
        for n, other in blocks
    ]
    return found + [
        pltpu.make_async_copy(ref.at[n], x_s.at[:, pl.ds(row_of(at, step, 1), 64), :], sem)
        for ref, blocks in zip(crossed, CROSS, strict=True)
        for n, step in blocks
    ]


def early_kernel(at, *refs):
    u_ref, out_ref, x_s, sem = refs[7:]
    copies = copies_early(at, refs[:7], x_s, sem)
    for c in copies:
        c.start()
    x_s[:, pl.ds(pl.multiple_of(lax.rem(at[0] + 4, 8) * 128, 128), 128), :] = jnp.zeros((2, 128, 512), BF)
    for c in copies:
        c.wait()
    for j in range(2):
        out_ref[j] = lax.dot_general(u_ref[j], x_s[j], (((0,), (0,)), ((), ())), preferred_element_type=F32)


def project_early(at, messages, u):
    return pl.pallas_call(
        early_kernel,
        out_shape=jax.ShapeDtypeStruct((2, 256, 512), F32),
        in_specs=[SMEM] + [ANY] * 7 + [VMEM],
        out_specs=VMEM,
        scratch_shapes=[pltpu.VMEM((2, 1024, 512), BF), pltpu.SemaphoreType.DMA(())],
        compiler_params=pltpu.CompilerParams(vmem_limit_bytes=16 << 20),
        cost_estimate=pl.CostEstimate(flops=2 * 2 * 256 * 1024 * 512, bytes_accessed=4 << 20, transcendentals=0),
        name="project_early",
    )(at, *messages, u)


def proj_kernel(at, rank, a_ref, b_ref, u_ref, early_ref, mine_ref, other_ref, x_s, u_s, sem):
    rows = pl.multiple_of(lax.rem(at[0] + 4, 8) * 128, 128)
    copies = [
        pltpu.make_async_copy(a_ref.at[0], x_s.at[:, pl.ds(pl.multiple_of(64 * at[1], 64), 64), :], sem),
        pltpu.make_async_copy(b_ref.at[0], x_s.at[:, pl.ds(pl.multiple_of(64 - 64 * at[1], 64), 64), :], sem),
        pltpu.make_async_copy(u_ref.at[:, pl.ds(rows, 128), :], u_s, sem),
    ]
    for c in copies:
        c.start()
    for c in copies:
        c.wait()
    slot = lax.broadcasted_iota(jnp.int32, (256, 1), 0)
    both = []
    for j in range(2):
        p = lax.dot_general(u_s[j], x_s[j], (((0,), (0,)), ((), ())), preferred_element_type=F32) + early_ref[j]
        both.append(jnp.where(slot < rank[2 * (2 * at[0] + at[1]) + j], p, 0.0))
    for y in range(4):
        a, b = (p[:, 128 * y : 128 * y + 128] for p in both)
        low = jnp.concatenate([a[:, :64], b[:, :64]], axis=-1).astype(BF)
        high = jnp.concatenate([a[:, 64:], b[:, 64:]], axis=-1).astype(BF)
        mine_ref[y] = jnp.where(at[3] == 0, low, high)
        other_ref[y] = jnp.where(at[3] == 0, high, low)


def project(at, panel_rank, a, b, u, early):
    return pl.pallas_call(
        proj_kernel,
        out_shape=(jax.ShapeDtypeStruct((4, 256, 128), BF),) * 2,
        in_specs=[SMEM, SMEM, ANY, ANY, ANY, VMEM],
        out_specs=(VMEM, VMEM),
        scratch_shapes=[
            pltpu.VMEM((2, 128, 512), BF),
            pltpu.VMEM((2, 128, 256), BF),
            pltpu.SemaphoreType.DMA(()),
        ],
        compiler_params=pltpu.CompilerParams(vmem_limit_bytes=4 << 20),
        cost_estimate=pl.CostEstimate(flops=2 * 2 * 256 * 128 * 512, bytes_accessed=2 << 20, transcendentals=0),
        name="project",
    )(at, panel_rank, a, b, u, early)


def part_kernel(p_ref, v_ref, out_ref):
    lane = lax.broadcasted_iota(jnp.int32, (1, 128), 1)
    p = p_ref[...]
    zero = jnp.zeros_like(p)
    s = jnp.dot(v_ref[0], jnp.where(lane < 64, p, zero), preferred_element_type=F32)
    s += jnp.dot(v_ref[1], jnp.where(lane < 64, zero, p), preferred_element_type=F32)
    s += jnp.concatenate([s[:, 64:], s[:, :64]], axis=-1)
    out_ref[...] = jnp.where(lane < 64, s[:512], s[512:]).astype(BF)


def sweep_part(p, v):
    return pl.pallas_call(
        part_kernel,
        out_shape=jax.ShapeDtypeStruct((512, 128), BF),
        in_specs=[VMEM, VMEM],
        out_specs=VMEM,
        compiler_params=pltpu.CompilerParams(vmem_limit_bytes=8 << 20),
        cost_estimate=pl.CostEstimate(flops=2 * 2 * 256 * 1024 * 128, bytes_accessed=2 << 20, transcendentals=0),
        name="sweep_part",
    )(p, v)


def base_kernel(at, rank_a, rank_b, *refs):
    messages, crossed = refs[:9], refs[9:13]
    qa, qb, pa, pb = refs[13:17]
    plus_ref, minus_ref, own_ref, next_ref, prev_ref = refs[17:22]
    x_s, q_s, p_s, t_s, stage, sem, q_sem, p_sem, o_sem = refs[22:]
    same = at[4] == at[1]
    x_copies = (
        copies_early(at, messages, x_s.at[0], sem.at[0]),
        copies_later(at, messages[:8], crossed, x_s.at[1], sem.at[1]),
    )

    def tile(ref, to, sems, h, i):
        return pltpu.make_async_copy(ref.at[i], to.at[2 * h + i], sems.at[2 * h + i])

    def fetch(h, a, b, to, sems):
        mine = same == (h == 0)

        @pl.when(mine)
        def _():
            for i in range(2):
                tile(a, to, sems, h, i).start()

        @pl.when(jnp.logical_not(mine))
        def _():
            for i in range(2):
                tile(b, to, sems, h, i).start()

    for h in range(2):
        for c in x_copies[h]:
            c.start()
        fetch(h, qa, qb, q_s, q_sem)
    for h in range(2):
        fetch(h, pa, pb, p_s, p_sem)
    slot = lax.broadcasted_iota(jnp.int32, (256, 1), 0)
    for h in range(2):
        mine = same == (h == 0)
        for c in x_copies[h]:
            c.wait()
        for i in range(2):
            tile(qa, q_s, q_sem, h, i).wait()
            for j in range(2):
                t = lax.dot_general(
                    q_s[2 * h + i, j], x_s[h, j], (((0,), (0,)), ((), ())), preferred_element_type=F32
                )
                rank = jnp.where(mine, rank_a[i, j], rank_b[i, j])
                t = jnp.where(slot < rank, t, 0.0).astype(BF)
                for y in range(4):
                    lanes = pl.multiple_of(lax.rem(y + 4 - at[2], 4) * 128, 128)
                    t_s[i, 2 * h + j, :, pl.ds(lanes, 128)] = t[:, 128 * y : 128 * y + 128]
    outs = (
        ((plus_ref.at[0], 2), (minus_ref.at[1], 3), (own_ref.at[0], 0), (next_ref, 1)),
        ((plus_ref.at[1], 1), (minus_ref.at[0], 2), (own_ref.at[1], 0), (prev_ref, 3)),
    )
    leaving = []
    for i in range(2):
        for h in range(2):
            tile(pa, p_s, p_sem, h, i).wait()
        for k in range(4):
            rows = slice(256 * k, 256 * k + 256)
            u = sum(
                jnp.dot(p_s[2 * h + i, j, rows], t_s[i, 2 * h + j], preferred_element_type=F32)
                for h in range(2)
                for j in range(2)
            )
            for n, (ref, d) in enumerate(outs[i]):
                stage[i, n, rows] = u[:, 128 * d : 128 * d + 128].astype(BF)
                leaving.append(pltpu.make_async_copy(stage.at[i, n, rows], ref.at[rows], o_sem))
                leaving[-1].start()
    for c in leaving:
        c.wait()


def base(at, rank_a, rank_b, *operands):
    two, one = (jax.ShapeDtypeStruct(n, BF) for n in ((2, 1024, 128), (1024, 128)))
    return pl.pallas_call(
        base_kernel,
        out_shape=(two, two, two, one, one),
        in_specs=[SMEM, SMEM, SMEM] + [ANY] * 17,
        out_specs=(ANY,) * 5,
        scratch_shapes=[
            pltpu.VMEM((2, 2, 1024, 512), BF),
            pltpu.VMEM((4, 2, 1024, 256), BF),
            pltpu.VMEM((4, 2, 1024, 256), BF),
            pltpu.VMEM((2, 4, 256, 512), BF),
            pltpu.VMEM((2, 4, 1024, 128), BF),
            pltpu.SemaphoreType.DMA((2,)),
            pltpu.SemaphoreType.DMA((4,)),
            pltpu.SemaphoreType.DMA((4,)),
            pltpu.SemaphoreType.DMA(()),
        ],
        compiler_params=pltpu.CompilerParams(vmem_limit_bytes=60 << 20),
        cost_estimate=pl.CostEstimate(flops=8 * 2 * 2 * 256 * 1024 * 512, bytes_accessed=15 << 20, transcendentals=0),
        name="base",
    )(at, rank_a, rank_b, *operands)


def pack_kernel(at, own_ref, plus_ref, minus_ref, low_ref, high_ref, keep_ref, send_ref):
    lane = lax.broadcasted_iota(jnp.int32, (1, 128), 1)
    a = own_ref[0].astype(F32) + minus_ref[1].astype(F32) + low_ref[...].astype(F32)
    b = own_ref[1].astype(F32) + plus_ref[1].astype(F32) + high_ref[...].astype(F32)
    turn = lambda v: jnp.concatenate([v[:, 64:], v[:, :64]], axis=-1)
    low = jnp.where(lane < 64, a, turn(b))
    high = jnp.where(lane < 64, turn(a), b)
    first = at[3] == 0
    keep_ref[...] = jnp.where(first, low, high)
    send_ref[...] = jnp.where(first, high, low).astype(BF)


def pack(at, own, plus, minus, low, high):
    return pl.pallas_call(
        pack_kernel,
        out_shape=(jax.ShapeDtypeStruct((1024, 128), F32), jax.ShapeDtypeStruct((1024, 128), BF)),
        in_specs=[SMEM] + [VMEM] * 5,
        out_specs=(VMEM, VMEM),
        compiler_params=pltpu.CompilerParams(vmem_limit_bytes=12 << 20),
        name="pack",
    )(at, own, plus, minus, low, high)


def last_kernel(at, rank, s_ref, u_ref, v_ref, keep_ref, came_ref, out_ref):
    lane = lax.broadcasted_iota(jnp.int32, (1, 128), 1)
    slot = lax.broadcasted_iota(jnp.int32, (256, 1), 0)
    packed = s_ref[...].astype(F32)
    turned = jnp.concatenate([packed[:, 64:], packed[:, :64]], axis=-1)
    s = jnp.concatenate([jnp.where(lane < 64, packed, turned), jnp.where(lane < 64, turned, packed)], axis=0)
    s = s.astype(BF)
    v = keep_ref[...] + came_ref[...].astype(F32)
    for i in range(2):
        back = lax.dot_general(v_ref[i], s, (((0,), (0,)), ((), ())), preferred_element_type=F32)
        keep = jnp.logical_and(slot < rank[2 * (2 * at[0] + at[1]) + i], (lane < 64) == (i == 0))
        back = jnp.where(keep, back, 0.0).astype(BF)
        v -= jnp.dot(u_ref[i], back, preferred_element_type=F32)
    t = v.T.astype(BF)
    out_ref[0] = t[:64]
    out_ref[1] = t[64:]


def last(at, panel_rank, s, u, v, keep, came):
    return pl.pallas_call(
        last_kernel,
        out_shape=jax.ShapeDtypeStruct((2, 64, 1024), BF),
        in_specs=[SMEM, SMEM] + [VMEM] * 5,
        out_specs=VMEM,
        compiler_params=pltpu.CompilerParams(vmem_limit_bytes=12 << 20),
        name="last",
    )(at, panel_rank, s, u, v, keep, came)


def panel_kernel(at, *refs):
    held, (u_ref, v_ref, sem) = refs[:8], refs[8:]
    copies = []
    for n, ref in enumerate(held):
        y = lax.rem(at[2] + n % 4, 4)
        co = at[4] if n < 4 else 1 - at[4]
        for m in range(2):
            xl = at[3] if m == 0 else 1 - at[3]
            rows = pl.multiple_of(y * 256 + xl * 128 + co * 64, 64)
            for f, out in enumerate((u_ref, v_ref)):
                copies.append(pltpu.make_async_copy(ref.at[m, f], out.at[:, pl.ds(rows, 64), :], sem))
    for c in copies:
        c.start()
    for c in copies:
        c.wait()


def whole_panel(at, u, v):
    both = jnp.stack([u, v])
    pair = jnp.stack([both, swap(both, "xl")])
    before = move(pair, "y", 1)
    after = move(pair, "y", -1)
    far = move(before, "y", 1)
    held = [pair, after, far, before]
    held += [swap(a, "co") for a in held]
    whole = jax.ShapeDtypeStruct((2, 1024, 256), BF)
    return pl.pallas_call(
        panel_kernel,
        out_shape=(whole, whole),
        in_specs=[SMEM] + [ANY] * 8,
        out_specs=(VMEM, ANY),
        scratch_shapes=[pltpu.SemaphoreType.DMA(())],
        compiler_params=pltpu.CompilerParams(vmem_limit_bytes=4 << 20),
        cost_estimate=pl.CostEstimate(flops=0, bytes_accessed=4 << 20, transcendentals=0),
        name="whole_panel",
    )(at, *held)


def shards(x_rhs, panel_u, panel_v, panel_rank, tile_p, tile_q, tile_rank):
    z, xh, y, xl, co = (lax.axis_index(a) for a in ALL)
    at = jnp.stack([z, xh, y, xl, co]).astype(jnp.int32)

    mine, theirs = split_columns(at, x_rhs)
    came = swap(theirs, "co")
    same = co == xh
    first, second = jnp.where(same, mine, came), jnp.where(same, came, mine)
    own = jnp.stack([first, second, swap(second, "xh")])
    p1, m1 = move(own, "z", 1), move(own, "z", -1)
    p2, m2 = move(p1, "z", 1), move(m1, "z", -1)
    p3, m3 = move(p2, "z", 1), move(m2, "z", -1)
    p4, m4 = move(p3[:2], "z", 1), move(m3[2:], "z", -1)
    messages = (own, p1, m1, p2, m2, p3, m3, p4, m4)
    crossed = (
        swap(jnp.stack([own[0], p1[0], m1[0]]), "xh"),
        swap(jnp.stack([p2[0], m2[0]]), "xh"),
        swap(jnp.stack([p3[0], m3[0]]), "xh"),
        swap(p4[:1], "xh"),
    )
    qb = swap(tile_q, "co")
    pb = swap(tile_p, "co")
    rank_b = swap(tile_rank, "co")
    u, v = whole_panel(at, panel_u, panel_v)

    early = project_early(at, messages[:7], u)
    row, other = project(at, panel_rank, p4, m4, u, early)
    n_z, n_h, n_y, n_l, n_c = (lax.axis_size(a) for a in ALL)

    def device(a, b, c, d, e):
        return (((a * n_h + b) * n_y + c) * n_l + d) * n_c + e

    spread = [(a, b, e) for a in range(n_z) for b in range(n_h) for e in range(n_c)]
    pairs = [(device(a, b, a >> 1, a & 1, e), device(a, b, a >> 1, 1 - (a & 1), e)) for a, b, e in spread]
    got = lax.ppermute(other, ALL, pairs)
    row = jnp.where(xl == lax.rem(z, 2), row, got)
    high = y // 2
    pairs = [
        (device(a, b, a >> 1, f, e), device(a, b, (a >> 1) ^ 2, f, e)) for a, b, e in spread for f in range(n_l)
    ]
    got = lax.ppermute(lax.dynamic_slice_in_dim(row, 2 - 2 * high, 2, 0), ALL, pairs)
    two = jnp.where(y == z // 2, lax.dynamic_slice_in_dim(row, 2 * high, 2, 0), got)
    low = lax.rem(y, 2)
    pairs = [
        (device(a, b, (a >> 1) ^ g, f, e), device(a, b, (a >> 1) ^ g ^ 1, f, e))
        for a, b, e in spread
        for f in range(n_l)
        for g in (0, 2)
    ]
    got = lax.ppermute(lax.dynamic_index_in_dim(two, 1 - low, 0, False), ALL, pairs)
    block = jnp.where(low == lax.rem(z // 2, 2), lax.dynamic_index_in_dim(two, low, 0, False), got)
    s = sweep_part(block, v)
    s = s + swap(s, "xh")
    right = move(s, "z", -1)
    pair = s + right
    near = pair + move(s, "z", 1)
    s = near + move(near, "z", -3) + move(pair, "z", 3)

    tiles = (tile_q, qb, tile_p, pb)
    operands = (*messages, *crossed, *tiles)
    plus, minus, own_sum, after, before = base(at, tile_rank, rank_b, *operands)
    plus, minus = move(plus, "y", 1), move(minus, "y", -1)
    up = move(after + plus[0], "y", 1)
    down = move(before + minus[0], "y", -1)
    keep, away = pack(at, own_sum, plus, minus, up, down)
    out = last(at, panel_rank, s, u, v, keep, swap(away, "xl"))
    return out.swapaxes(1, 2)


def solution(mesh):
    finer = Mesh(mesh.devices.reshape(8, 2, 4, 2, 2), ALL)
    return jax.shard_map(
        shards,
        mesh=finer,
        in_specs=(
            P(COL, ROW, None),
            P(ROW, COL, None),
            P(ROW, COL, None),
            P(),
            P(ROW, COL, None, None),
            P(ROW, COL, None, None),
            P(ROW, COL),
        ),
        out_specs=P(ROW, None, COL),
        check_vma=False,
    )
```

```python
import functools

import jax
import jax.numpy as jnp
from jax import lax
from jax.experimental import pallas as pl
from jax.experimental.pallas import tpu as pltpu
from jax.sharding import Mesh
from jax.sharding import PartitionSpec as P

ALL = ("z", "xh", "y", "xl", "co")
ROW = ("z", "xh")
COL = ("y", "xl", "co")
BF = jnp.bfloat16
F32 = jnp.float32
ANY = pl.BlockSpec(memory_space=pl.ANY)
SMEM = pl.BlockSpec(memory_space=pltpu.SMEM)
VMEM = pl.BlockSpec(memory_space=pltpu.VMEM)


def move(a, axis, k):
    n = lax.axis_size(axis)
    return lax.ppermute(a, axis, [(i, (i + k) % n) for i in range(n)])


def swap(a, axis, k=1):
    n = lax.axis_size(axis)
    return lax.ppermute(a, axis, [(i, i ^ k) for i in range(n)])


def split_kernel(at, x_ref, mine_ref, theirs_ref):
    first = at[4] == 0
    for y in range(4):
        a = x_ref[:, :, 256 * y : 256 * y + 128]
        b = x_ref[:, :, 256 * y + 128 : 256 * y + 256]
        low = jnp.concatenate([a[..., :64], b[..., :64]], axis=-1)
        high = jnp.concatenate([a[..., 64:], b[..., 64:]], axis=-1)
        mine_ref[:, :, 128 * y : 128 * y + 128] = jnp.where(first, low, high)
        theirs_ref[:, :, 128 * y : 128 * y + 128] = jnp.where(first, high, low)


def split_columns(at, x):
    half = jax.ShapeDtypeStruct((2, 64, 512), BF)
    return pl.pallas_call(
        split_kernel,
        out_shape=(half, half),
        in_specs=[SMEM, VMEM],
        out_specs=(VMEM, VMEM),
        compiler_params=pltpu.CompilerParams(vmem_limit_bytes=8 << 20),
        name="split_columns",
    )(at, x)


EARLY = tuple((step, ((0, 0), (2, 1))) for step in (0, -1, 1, -2, 2, -3, 3))
LATER = (0, -1, 1, -2, 2, -3, 3)
CROSS = (((0, 0), (1, -1), (2, 1)), ((0, -2), (1, 2)), ((0, -3), (1, 3)), ((0, 4),))


def row_of(at, step, other):
    rows = lax.rem(at[0] + step + 8, 8) * 128 + (1 - at[1] if other else at[1]) * 64
    return pl.multiple_of(rows, 64)


def copies_early(at, refs, x_s, sem):
    found = [
        pltpu.make_async_copy(ref.at[n], x_s.at[:, pl.ds(row_of(at, step, other), 64), :], sem)
        for ref, (step, blocks) in zip(refs[:7], EARLY, strict=True)
        for n, other in blocks
    ]
    if len(refs) == 9:
        found += [
            pltpu.make_async_copy(ref.at[n : n + 2], x_s.at[:, pl.ds(row_of(at, 4, other), 64), :], sem)
            for ref, n, other in ((refs[7], 0, 0), (refs[8], 1, 1))
        ]
    return found


def copies_later(at, refs, crossed, x_s, sem):
    found = [
        pltpu.make_async_copy(ref.at[1], x_s.at[:, pl.ds(row_of(at, step, 0), 64), :], sem)
        for ref, step in zip(refs[:7], LATER, strict=True)
    ]
    found += [
        pltpu.make_async_copy(ref.at[n], x_s.at[j, pl.ds(row_of(at, 4, 0), 64), :], sem)
        for j, (ref, n) in enumerate(((refs[7], 2), (refs[8], 0)))
    ]
    return found + [
        pltpu.make_async_copy(ref.at[n], x_s.at[:, pl.ds(row_of(at, step, 1), 64), :], sem)
        for ref, blocks in zip(crossed, CROSS, strict=True)
        for n, step in blocks
    ]


def early_kernel(at, *refs):
    u_ref, out_ref, x_s, sem = refs[7:]
    copies = copies_early(at, refs[:7], x_s, sem)
    for c in copies:
        c.start()
    x_s[:, pl.ds(pl.multiple_of(lax.rem(at[0] + 4, 8) * 128, 128), 128), :] = jnp.zeros((2, 128, 512), BF)
    for c in copies:
        c.wait()
    for j in range(2):
        out_ref[j] = lax.dot_general(u_ref[j], x_s[j], (((0,), (0,)), ((), ())), preferred_element_type=F32)


def project_early(at, messages, u):
    return pl.pallas_call(
        early_kernel,
        out_shape=jax.ShapeDtypeStruct((2, 256, 512), F32),
        in_specs=[SMEM] + [ANY] * 7 + [VMEM],
        out_specs=VMEM,
        scratch_shapes=[pltpu.VMEM((2, 1024, 512), BF), pltpu.SemaphoreType.DMA(())],
        compiler_params=pltpu.CompilerParams(vmem_limit_bytes=16 << 20),
        cost_estimate=pl.CostEstimate(flops=2 * 2 * 256 * 1024 * 512, bytes_accessed=4 << 20, transcendentals=0),
        name="project_early",
    )(at, *messages, u)


def proj_kernel(at, rank, a_ref, b_ref, u_ref, early_ref, mine_ref, other_ref, x_s, u_s, sem):
    rows = pl.multiple_of(lax.rem(at[0] + 4, 8) * 128, 128)
    copies = [
        pltpu.make_async_copy(a_ref.at[0:2], x_s.at[:, pl.ds(pl.multiple_of(64 * at[1], 64), 64), :], sem),
        pltpu.make_async_copy(b_ref.at[1:3], x_s.at[:, pl.ds(pl.multiple_of(64 - 64 * at[1], 64), 64), :], sem),
        pltpu.make_async_copy(u_ref.at[:, pl.ds(rows, 128), :], u_s, sem),
    ]
    for c in copies:
        c.start()
    for c in copies:
        c.wait()
    slot = lax.broadcasted_iota(jnp.int32, (256, 1), 0)
    both = []
    for j in range(2):
        p = lax.dot_general(u_s[j], x_s[j], (((0,), (0,)), ((), ())), preferred_element_type=F32) + early_ref[j]
        both.append(jnp.where(slot < rank[2 * (2 * at[0] + at[1]) + j], p, 0.0))
    for y in range(4):
        a, b = (p[:, 128 * y : 128 * y + 128] for p in both)
        low = jnp.concatenate([a[:, :64], b[:, :64]], axis=-1).astype(BF)
        high = jnp.concatenate([a[:, 64:], b[:, 64:]], axis=-1).astype(BF)
        mine_ref[y] = jnp.where(at[3] == 0, low, high)
        other_ref[y] = jnp.where(at[3] == 0, high, low)


def project(at, panel_rank, a, b, u, early):
    return pl.pallas_call(
        proj_kernel,
        out_shape=(jax.ShapeDtypeStruct((4, 256, 128), BF),) * 2,
        in_specs=[SMEM, SMEM, ANY, ANY, ANY, VMEM],
        out_specs=(VMEM, VMEM),
        scratch_shapes=[
            pltpu.VMEM((2, 128, 512), BF),
            pltpu.VMEM((2, 128, 256), BF),
            pltpu.SemaphoreType.DMA(()),
        ],
        compiler_params=pltpu.CompilerParams(vmem_limit_bytes=4 << 20),
        cost_estimate=pl.CostEstimate(flops=2 * 2 * 256 * 128 * 512, bytes_accessed=2 << 20, transcendentals=0),
        name="project",
    )(at, panel_rank, a, b, u, early)


def part_kernel(p_ref, v_ref, out_ref):
    lane = lax.broadcasted_iota(jnp.int32, (1, 128), 1)
    p = p_ref[...]
    zero = jnp.zeros_like(p)
    s = jnp.dot(v_ref[0], jnp.where(lane < 64, p, zero), preferred_element_type=F32)
    s += jnp.dot(v_ref[1], jnp.where(lane < 64, zero, p), preferred_element_type=F32)
    s += jnp.concatenate([s[:, 64:], s[:, :64]], axis=-1)
    out_ref[...] = jnp.where(lane < 64, s[:512], s[512:]).astype(BF)


def sweep_part(p, v):
    return pl.pallas_call(
        part_kernel,
        out_shape=jax.ShapeDtypeStruct((512, 128), BF),
        in_specs=[VMEM, VMEM],
        out_specs=VMEM,
        compiler_params=pltpu.CompilerParams(vmem_limit_bytes=8 << 20),
        cost_estimate=pl.CostEstimate(flops=2 * 2 * 256 * 1024 * 128, bytes_accessed=2 << 20, transcendentals=0),
        name="sweep_part",
    )(p, v)


def base_kernel(i, at, rank_a, rank_b, *refs):
    messages, crossed = refs[:9], refs[9:13]
    qa, qb, pa, pb = refs[13:17]
    refs = refs[17:] if i == 0 else refs[20:]
    plus_ref, minus_ref, own_ref, side_ref, x_s, q_s, p_s, t_s, stage, sem, q_sem, p_sem, o_sem = refs
    same = at[4] == at[1]
    x_copies = (
        copies_early(at, messages, x_s.at[0], sem.at[0]),
        copies_later(at, messages, crossed, x_s.at[1], sem.at[1]),
    )

    def tile(ref, to, sems, h):
        return pltpu.make_async_copy(ref.at[i], to.at[h], sems.at[h])

    def fetch(h, a, b, to, sems):
        mine = same == (h == 0)

        @pl.when(mine)
        def _():
            tile(a, to, sems, h).start()

        @pl.when(jnp.logical_not(mine))
        def _():
            tile(b, to, sems, h).start()

    for h in range(2):
        for c in x_copies[h]:
            c.start()
        fetch(h, qa, qb, q_s, q_sem)
    for h in range(2):
        fetch(h, pa, pb, p_s, p_sem)
    slot = lax.broadcasted_iota(jnp.int32, (256, 1), 0)
    for h in range(2):
        mine = same == (h == 0)
        for c in x_copies[h]:
            c.wait()
        tile(qa, q_s, q_sem, h).wait()
        for j in range(2):
            t = lax.dot_general(q_s[h, j], x_s[h, j], (((0,), (0,)), ((), ())), preferred_element_type=F32)
            rank = jnp.where(mine, rank_a[i, j], rank_b[i, j])
            t = jnp.where(slot < rank, t, 0.0).astype(BF)
            for y in range(4):
                lanes = pl.multiple_of(lax.rem(y + 4 - at[2], 4) * 128, 128)
                t_s[2 * h + j, :, pl.ds(lanes, 128)] = t[:, 128 * y : 128 * y + 128]
    outs = (
        ((plus_ref.at[0], 2), (minus_ref.at[1], 3), (own_ref.at[0], 0), (side_ref, 1))
        if i == 0
        else ((plus_ref.at[1], 1), (minus_ref.at[0], 2), (own_ref.at[1], 0), (side_ref, 3))
    )
    leaving = []
    for h in range(2):
        tile(pa, p_s, p_sem, h).wait()
    for k in range(4):
        rows = slice(256 * k, 256 * k + 256)
        u = sum(
            jnp.dot(p_s[h, j, rows], t_s[2 * h + j], preferred_element_type=F32) for h in range(2) for j in range(2)
        )
        for n, (ref, d) in enumerate(outs):
            stage[n, rows] = u[:, 128 * d : 128 * d + 128].astype(BF)
            leaving.append(pltpu.make_async_copy(stage.at[n, rows], ref.at[rows], o_sem))
            leaving[-1].start()
    for c in leaving:
        c.wait()


def base(i, at, rank_a, rank_b, *operands):
    two, one = (jax.ShapeDtypeStruct(n, BF) for n in ((2, 1024, 128), (1024, 128)))
    return pl.pallas_call(
        functools.partial(base_kernel, i),
        out_shape=(two, two, two, one),
        in_specs=[SMEM, SMEM, SMEM] + [ANY] * len(operands),
        out_specs=(ANY,) * 4,
        scratch_shapes=[
            pltpu.VMEM((2, 2, 1024, 512), BF),
            pltpu.VMEM((2, 2, 1024, 256), BF),
            pltpu.VMEM((2, 2, 1024, 256), BF),
            pltpu.VMEM((4, 256, 512), BF),
            pltpu.VMEM((4, 1024, 128), BF),
            pltpu.SemaphoreType.DMA((2,)),
            pltpu.SemaphoreType.DMA((2,)),
            pltpu.SemaphoreType.DMA((2,)),
            pltpu.SemaphoreType.DMA(()),
        ],
        input_output_aliases={20: 0, 21: 1, 22: 2} if i == 1 else {},
        compiler_params=pltpu.CompilerParams(vmem_limit_bytes=60 << 20),
        cost_estimate=pl.CostEstimate(flops=4 * 2 * 2 * 256 * 1024 * 512, bytes_accessed=9 << 20, transcendentals=0),
    )(at, rank_a, rank_b, *operands)


def pack_kernel(at, own_ref, plus_ref, minus_ref, low_ref, high_ref, keep_ref, send_ref):
    lane = lax.broadcasted_iota(jnp.int32, (1, 128), 1)
    a = own_ref[0].astype(F32) + minus_ref[1].astype(F32) + low_ref[...].astype(F32)
    b = own_ref[1].astype(F32) + plus_ref[1].astype(F32) + high_ref[...].astype(F32)
    turn = lambda v: jnp.concatenate([v[:, 64:], v[:, :64]], axis=-1)
    low = jnp.where(lane < 64, a, turn(b))
    high = jnp.where(lane < 64, turn(a), b)
    first = at[3] == 0
    keep_ref[...] = jnp.where(first, low, high)
    send_ref[...] = jnp.where(first, high, low).astype(BF)


def pack(at, own, plus, minus, low, high):
    return pl.pallas_call(
        pack_kernel,
        out_shape=(jax.ShapeDtypeStruct((1024, 128), F32), jax.ShapeDtypeStruct((1024, 128), BF)),
        in_specs=[SMEM] + [VMEM] * 5,
        out_specs=(VMEM, VMEM),
        compiler_params=pltpu.CompilerParams(vmem_limit_bytes=12 << 20),
        name="pack",
    )(at, own, plus, minus, low, high)


def late_kernel(at, rank, s_ref, u_ref, v_ref, out_ref):
    lane = lax.broadcasted_iota(jnp.int32, (1, 128), 1)
    slot = lax.broadcasted_iota(jnp.int32, (256, 1), 0)
    packed = s_ref[...].astype(F32)
    turned = jnp.concatenate([packed[:, 64:], packed[:, :64]], axis=-1)
    s = jnp.concatenate([jnp.where(lane < 64, packed, turned), jnp.where(lane < 64, turned, packed)], axis=0)
    s = s.astype(BF)
    total = []
    for i in range(2):
        back = lax.dot_general(v_ref[i], s, (((0,), (0,)), ((), ())), preferred_element_type=F32)
        keep = jnp.logical_and(slot < rank[2 * (2 * at[0] + at[1]) + i], (lane < 64) == (i == 0))
        back = jnp.where(keep, back, 0.0).astype(BF)
        total.append(jnp.dot(u_ref[i], back, preferred_element_type=F32))
    out_ref[...] = total[0] + total[1]


def late(at, panel_rank, s, u, v):
    return pl.pallas_call(
        late_kernel,
        out_shape=jax.ShapeDtypeStruct((1024, 128), F32),
        in_specs=[SMEM, SMEM, VMEM, VMEM, VMEM],
        out_specs=VMEM,
        compiler_params=pltpu.CompilerParams(vmem_limit_bytes=12 << 20),
        cost_estimate=pl.CostEstimate(flops=4 * 2 * 256 * 1024 * 128, bytes_accessed=3 << 20, transcendentals=0),
        name="late",
    )(at, panel_rank, s, u, v)


def last_kernel(keep_ref, came_ref, late_ref, out_ref):
    v = keep_ref[...] + came_ref[...].astype(F32) - late_ref[...]
    t = v.T.astype(BF)
    out_ref[0] = t[:64]
    out_ref[1] = t[64:]


def last(keep, came, correction):
    return pl.pallas_call(
        last_kernel,
        out_shape=jax.ShapeDtypeStruct((2, 64, 1024), BF),
        in_specs=[VMEM] * 3,
        out_specs=VMEM,
        compiler_params=pltpu.CompilerParams(vmem_limit_bytes=8 << 20),
        name="last",
    )(keep, came, correction)


def panel_kernel(at, *refs):
    held, (u_ref, v_ref, sem) = refs[:8], refs[8:]
    copies = []
    for n, ref in enumerate(held):
        y = lax.rem(at[2] + n % 4, 4)
        co = at[4] if n < 4 else 1 - at[4]
        for m in range(2):
            xl = at[3] if m == 0 else 1 - at[3]
            rows = pl.multiple_of(y * 256 + xl * 128 + co * 64, 64)
            for f, out in enumerate((u_ref, v_ref)):
                copies.append(pltpu.make_async_copy(ref.at[m, f], out.at[:, pl.ds(rows, 64), :], sem))
    for c in copies:
        c.start()
    for c in copies:
        c.wait()


def whole_panel(at, u, v):
    both = jnp.stack([u, v])
    pair = jnp.stack([both, swap(both, "xl")])
    before = move(pair, "y", 1)
    after = move(pair, "y", -1)
    far = move(before, "y", 1)
    held = [pair, after, far, before]
    held += [swap(a, "co") for a in held]
    whole = jax.ShapeDtypeStruct((2, 1024, 256), BF)
    return pl.pallas_call(
        panel_kernel,
        out_shape=(whole, whole),
        in_specs=[SMEM] + [ANY] * 8,
        out_specs=(VMEM, ANY),
        scratch_shapes=[pltpu.SemaphoreType.DMA(())],
        compiler_params=pltpu.CompilerParams(vmem_limit_bytes=4 << 20),
        cost_estimate=pl.CostEstimate(flops=0, bytes_accessed=4 << 20, transcendentals=0),
        name="whole_panel",
    )(at, *held)


def shards(x_rhs, panel_u, panel_v, panel_rank, tile_p, tile_q, tile_rank):
    z, xh, y, xl, co = (lax.axis_index(a) for a in ALL)
    at = jnp.stack([z, xh, y, xl, co]).astype(jnp.int32)

    mine, theirs = split_columns(at, x_rhs)
    came = swap(theirs, "co")
    same = co == xh
    first, second = jnp.where(same, mine, came), jnp.where(same, came, mine)
    own = jnp.stack([first, second, swap(second, "xh")])
    p1, m1 = move(own, "z", 1), move(own, "z", -1)
    p2, m2 = move(p1, "z", 1), move(m1, "z", -1)
    p3, m3 = move(p2, "z", 1), move(m2, "z", -1)
    p4, m4 = move(p3.reshape(6, 64, 512)[:3], "z", 1), move(m3.reshape(6, 64, 512)[3:], "z", -1)
    messages = (own, p1, m1, p2, m2, p3, m3, p4, m4)
    crossed = (
        swap(jnp.stack([own[0], p1[0], m1[0]]), "xh"),
        swap(jnp.stack([p2[0], m2[0]]), "xh"),
        swap(jnp.stack([p3[0], m3[0]]), "xh"),
        swap(p4[None, :2], "xh"),
    )
    qb = swap(tile_q, "co")
    pb = swap(tile_p, "co")
    rank_b = swap(tile_rank, "co")
    u, v = whole_panel(at, panel_u, panel_v)

    early = project_early(at, messages[:7], u)
    row, other = project(at, panel_rank, p4, m4, u, early)
    got = swap(other, "xl")
    row = jnp.where(xl == lax.rem(z, 2), row, got)
    high = y // 2
    got = swap(lax.dynamic_slice_in_dim(row, 2 - 2 * high, 2, 0), "y", 2)
    two = jnp.where(y == z // 2, lax.dynamic_slice_in_dim(row, 2 * high, 2, 0), got)
    low = lax.rem(y, 2)
    got = swap(lax.dynamic_index_in_dim(two, 1 - low, 0, False), "y", 1)
    block = jnp.where(low == lax.rem(z // 2, 2), lax.dynamic_index_in_dim(two, low, 0, False), got)
    s = sweep_part(block, v)
    s = s + swap(s, "xh")
    right = move(s, "z", -1)
    pair = s + right
    near = pair + move(s, "z", 1)
    s = near + move(near, "z", -3) + move(pair, "z", 3)

    tiles = (tile_q, qb, tile_p, pb)
    operands = (*messages, *crossed, *tiles)
    plus, minus, own_sum, after = base(0, at, tile_rank, rank_b, *operands)
    plus, minus, own_sum, before = base(1, at, tile_rank, rank_b, *operands, plus, minus, own_sum)
    plus, minus = move(plus, "y", 1), move(minus, "y", -1)
    up = move(after + plus[0], "y", 1)
    down = move(before + minus[0], "y", -1)
    keep, away = pack(at, own_sum, plus, minus, up, down)
    came = swap(away, "xl")
    correction = late(at, panel_rank, s, u, v)
    out = last(keep, came, correction)
    return out.swapaxes(1, 2)


def solution(mesh):
    finer = Mesh(mesh.devices.reshape(8, 2, 4, 2, 2), ALL)
    return jax.shard_map(
        shards,
        mesh=finer,
        in_specs=(
            P(COL, ROW, None),
            P(ROW, COL, None),
            P(ROW, COL, None),
            P(),
            P(ROW, COL, None, None),
            P(ROW, COL, None, None),
            P(ROW, COL),
        ),
        out_specs=P(ROW, None, COL),
        check_vma=False,
    )
```

```python
import functools

import jax
import jax.numpy as jnp
from jax import lax
from jax.experimental import pallas as pl
from jax.experimental.pallas import tpu as pltpu
from jax.sharding import Mesh
from jax.sharding import PartitionSpec as P

ALL = ("z", "xh", "y", "xl", "co")
ROW = ("z", "xh")
COL = ("y", "xl", "co")
BF = jnp.bfloat16
F32 = jnp.float32
ANY = pl.BlockSpec(memory_space=pl.ANY)
SMEM = pl.BlockSpec(memory_space=pltpu.SMEM)
VMEM = pl.BlockSpec(memory_space=pltpu.VMEM)


def move(a, axis, k):
    n = lax.axis_size(axis)
    return lax.ppermute(a, axis, [(i, (i + k) % n) for i in range(n)])


def swap(a, axis, k=1):
    n = lax.axis_size(axis)
    return lax.ppermute(a, axis, [(i, i ^ k) for i in range(n)])


def split_kernel(at, x_ref, mine_ref, theirs_ref):
    first = at[4] == 0
    for y in range(4):
        a = x_ref[:, :, 256 * y : 256 * y + 128]
        b = x_ref[:, :, 256 * y + 128 : 256 * y + 256]
        low = jnp.concatenate([a[..., :64], b[..., :64]], axis=-1)
        high = jnp.concatenate([a[..., 64:], b[..., 64:]], axis=-1)
        mine_ref[:, :, 128 * y : 128 * y + 128] = jnp.where(first, low, high)
        theirs_ref[:, :, 128 * y : 128 * y + 128] = jnp.where(first, high, low)


def split_columns(at, x):
    half = jax.ShapeDtypeStruct((2, 64, 512), BF)
    return pl.pallas_call(
        split_kernel,
        out_shape=(half, half),
        in_specs=[SMEM, VMEM],
        out_specs=(VMEM, VMEM),
        compiler_params=pltpu.CompilerParams(vmem_limit_bytes=8 << 20),
        name="split_columns",
    )(at, x)


EARLY = tuple((step, ((0, 0), (2, 1))) for step in (0, -1, 1, -2, 2, -3, 3))
LATER = (0, -1, 1, -2, 2, -3, 3)
CROSS = (((0, 0), (1, -1), (2, 1)), ((0, -2), (1, 2)), ((0, -3), (1, 3)), ((0, 4),))


def row_of(at, step, other):
    rows = lax.rem(at[0] + step + 8, 8) * 128 + (1 - at[1] if other else at[1]) * 64
    return pl.multiple_of(rows, 64)


def copies_early(at, refs, x_s, sem):
    found = [
        pltpu.make_async_copy(ref.at[n], x_s.at[:, pl.ds(row_of(at, step, other), 64), :], sem)
        for ref, (step, blocks) in zip(refs[:7], EARLY, strict=True)
        for n, other in blocks
    ]
    if len(refs) == 9:
        found += [
            pltpu.make_async_copy(ref.at[n : n + 2], x_s.at[:, pl.ds(row_of(at, 4, other), 64), :], sem)
            for ref, n, other in ((refs[7], 0, 0), (refs[8], 1, 1))
        ]
    return found


def copies_later(at, refs, crossed, x_s, sem):
    found = [
        pltpu.make_async_copy(ref.at[1], x_s.at[:, pl.ds(row_of(at, step, 0), 64), :], sem)
        for ref, step in zip(refs[:7], LATER, strict=True)
    ]
    found += [
        pltpu.make_async_copy(ref.at[n], x_s.at[j, pl.ds(row_of(at, 4, 0), 64), :], sem)
        for j, (ref, n) in enumerate(((refs[7], 2), (refs[8], 0)))
    ]
    return found + [
        pltpu.make_async_copy(ref.at[n], x_s.at[:, pl.ds(row_of(at, step, 1), 64), :], sem)
        for ref, blocks in zip(crossed, CROSS, strict=True)
        for n, step in blocks
    ]


def early_kernel(at, *refs):
    u_ref, out_ref, x_s, sem = refs[7:]
    copies = copies_early(at, refs[:7], x_s, sem)
    for c in copies:
        c.start()
    x_s[:, pl.ds(pl.multiple_of(lax.rem(at[0] + 4, 8) * 128, 128), 128), :] = jnp.zeros((2, 128, 512), BF)
    for c in copies:
        c.wait()
    for j in range(2):
        out_ref[j] = lax.dot_general(u_ref[j], x_s[j], (((0,), (0,)), ((), ())), preferred_element_type=F32)


def project_early(at, messages, u):
    return pl.pallas_call(
        early_kernel,
        out_shape=jax.ShapeDtypeStruct((2, 256, 512), F32),
        in_specs=[SMEM] + [ANY] * 7 + [VMEM],
        out_specs=VMEM,
        scratch_shapes=[pltpu.VMEM((2, 1024, 512), BF), pltpu.SemaphoreType.DMA(())],
        compiler_params=pltpu.CompilerParams(vmem_limit_bytes=16 << 20),
        cost_estimate=pl.CostEstimate(flops=2 * 2 * 256 * 1024 * 512, bytes_accessed=4 << 20, transcendentals=0),
        name="project_early",
    )(at, *messages, u)


def proj_kernel(at, rank, a_ref, b_ref, u_ref, early_ref, mine_ref, other_ref, x_s, u_s, sem):
    rows = pl.multiple_of(lax.rem(at[0] + 4, 8) * 128, 128)
    copies = [
        pltpu.make_async_copy(a_ref.at[0:2], x_s.at[:, pl.ds(pl.multiple_of(64 * at[1], 64), 64), :], sem),
        pltpu.make_async_copy(b_ref.at[1:3], x_s.at[:, pl.ds(pl.multiple_of(64 - 64 * at[1], 64), 64), :], sem),
        pltpu.make_async_copy(u_ref.at[:, pl.ds(rows, 128), :], u_s, sem),
    ]
    for c in copies:
        c.start()
    for c in copies:
        c.wait()
    slot = lax.broadcasted_iota(jnp.int32, (256, 1), 0)
    both = []
    for j in range(2):
        p = lax.dot_general(u_s[j], x_s[j], (((0,), (0,)), ((), ())), preferred_element_type=F32) + early_ref[j]
        both.append(jnp.where(slot < rank[2 * (2 * at[0] + at[1]) + j], p, 0.0))
    for y in range(4):
        a, b = (p[:, 128 * y : 128 * y + 128] for p in both)
        low = jnp.concatenate([a[:, :64], b[:, :64]], axis=-1).astype(BF)
        high = jnp.concatenate([a[:, 64:], b[:, 64:]], axis=-1).astype(BF)
        mine_ref[y] = jnp.where(at[3] == 0, low, high)
        other_ref[y] = jnp.where(at[3] == 0, high, low)


def project(at, panel_rank, a, b, u, early):
    return pl.pallas_call(
        proj_kernel,
        out_shape=(jax.ShapeDtypeStruct((4, 256, 128), BF),) * 2,
        in_specs=[SMEM, SMEM, ANY, ANY, ANY, VMEM],
        out_specs=(VMEM, VMEM),
        scratch_shapes=[
            pltpu.VMEM((2, 128, 512), BF),
            pltpu.VMEM((2, 128, 256), BF),
            pltpu.SemaphoreType.DMA(()),
        ],
        compiler_params=pltpu.CompilerParams(vmem_limit_bytes=4 << 20),
        cost_estimate=pl.CostEstimate(flops=2 * 2 * 256 * 128 * 512, bytes_accessed=2 << 20, transcendentals=0),
        name="project",
    )(at, panel_rank, a, b, u, early)


def part_kernel(at, held_ref, got_ref, v_ref, out_ref):
    lane = lax.broadcasted_iota(jnp.int32, (1, 128), 1)
    p = jnp.where(lax.rem(at[2], 2) == lax.rem(at[0] // 2, 2), held_ref[...], got_ref[...])
    zero = jnp.zeros_like(p)
    s = jnp.dot(v_ref[0], jnp.where(lane < 64, p, zero), preferred_element_type=F32)
    s += jnp.dot(v_ref[1], jnp.where(lane < 64, zero, p), preferred_element_type=F32)
    s += jnp.concatenate([s[:, 64:], s[:, :64]], axis=-1)
    out_ref[...] = jnp.where(lane < 64, s[:512], s[512:]).astype(BF)


def sweep_part(at, held, got, v):
    return pl.pallas_call(
        part_kernel,
        out_shape=jax.ShapeDtypeStruct((512, 128), BF),
        in_specs=[SMEM, VMEM, VMEM, VMEM],
        out_specs=VMEM,
        compiler_params=pltpu.CompilerParams(vmem_limit_bytes=8 << 20),
        cost_estimate=pl.CostEstimate(flops=2 * 2 * 256 * 1024 * 128, bytes_accessed=2 << 20, transcendentals=0),
        name="sweep_part",
    )(at, held, got, v)


def base_kernel(i, at, rank_a, rank_b, *refs):
    messages, crossed = refs[:9], refs[9:13]
    qa, qb, pa, pb = refs[13:17]
    refs = refs[17:] if i == 0 else refs[20:]
    plus_ref, minus_ref, own_ref, side_ref, x_s, q_s, p_s, t_s, stage, sem, q_sem, p_sem, o_sem = refs
    same = at[4] == at[1]
    x_copies = (
        copies_early(at, messages, x_s.at[0], sem.at[0]),
        copies_later(at, messages, crossed, x_s.at[1], sem.at[1]),
    )

    def tile(ref, to, sems, h):
        return pltpu.make_async_copy(ref.at[i], to.at[h], sems.at[h])

    def fetch(h, a, b, to, sems):
        mine = same == (h == 0)

        @pl.when(mine)
        def _():
            tile(a, to, sems, h).start()

        @pl.when(jnp.logical_not(mine))
        def _():
            tile(b, to, sems, h).start()

    for h in range(2):
        for c in x_copies[h]:
            c.start()
        fetch(h, qa, qb, q_s, q_sem)
    for h in range(2):
        fetch(h, pa, pb, p_s, p_sem)
    slot = lax.broadcasted_iota(jnp.int32, (256, 1), 0)
    for h in range(2):
        mine = same == (h == 0)
        for c in x_copies[h]:
            c.wait()
        tile(qa, q_s, q_sem, h).wait()
        for j in range(2):
            t = lax.dot_general(q_s[h, j], x_s[h, j], (((0,), (0,)), ((), ())), preferred_element_type=F32)
            rank = jnp.where(mine, rank_a[i, j], rank_b[i, j])
            t = jnp.where(slot < rank, t, 0.0).astype(BF)
            for y in range(4):
                lanes = pl.multiple_of(lax.rem(y + 4 - at[2], 4) * 128, 128)
                t_s[2 * h + j, :, pl.ds(lanes, 128)] = t[:, 128 * y : 128 * y + 128]
    outs = (
        ((plus_ref.at[0], 2), (minus_ref.at[1], 3), (own_ref.at[0], 0), (side_ref, 1))
        if i == 0
        else ((plus_ref.at[1], 1), (minus_ref.at[0], 2), (own_ref.at[1], 0), (side_ref, 3))
    )
    leaving = []
    for h in range(2):
        tile(pa, p_s, p_sem, h).wait()
    for k in range(4):
        rows = slice(256 * k, 256 * k + 256)
        u = sum(
            jnp.dot(p_s[h, j, rows], t_s[2 * h + j], preferred_element_type=F32) for h in range(2) for j in range(2)
        )
        for n, (ref, d) in enumerate(outs):
            stage[n, rows] = u[:, 128 * d : 128 * d + 128].astype(BF)
            leaving.append(pltpu.make_async_copy(stage.at[n, rows], ref.at[rows], o_sem))
            leaving[-1].start()
    for c in leaving:
        c.wait()


def base(i, at, rank_a, rank_b, *operands):
    two, one = (jax.ShapeDtypeStruct(n, BF) for n in ((2, 1024, 128), (1024, 128)))
    return pl.pallas_call(
        functools.partial(base_kernel, i),
        out_shape=(two, two, two, one),
        in_specs=[SMEM, SMEM, SMEM] + [ANY] * len(operands),
        out_specs=(ANY,) * 4,
        scratch_shapes=[
            pltpu.VMEM((2, 2, 1024, 512), BF),
            pltpu.VMEM((2, 2, 1024, 256), BF),
            pltpu.VMEM((2, 2, 1024, 256), BF),
            pltpu.VMEM((4, 256, 512), BF),
            pltpu.VMEM((4, 1024, 128), BF),
            pltpu.SemaphoreType.DMA((2,)),
            pltpu.SemaphoreType.DMA((2,)),
            pltpu.SemaphoreType.DMA((2,)),
            pltpu.SemaphoreType.DMA(()),
        ],
        input_output_aliases={20: 0, 21: 1, 22: 2} if i == 1 else {},
        compiler_params=pltpu.CompilerParams(vmem_limit_bytes=60 << 20),
        cost_estimate=pl.CostEstimate(flops=4 * 2 * 2 * 256 * 1024 * 512, bytes_accessed=9 << 20, transcendentals=0),
    )(at, rank_a, rank_b, *operands)


def pack_kernel(at, own_ref, plus_ref, minus_ref, low_ref, high_ref, keep_ref, send_ref):
    lane = lax.broadcasted_iota(jnp.int32, (1, 128), 1)
    a = own_ref[0].astype(F32) + minus_ref[1].astype(F32) + low_ref[...].astype(F32)
    b = own_ref[1].astype(F32) + plus_ref[1].astype(F32) + high_ref[...].astype(F32)
    turn = lambda v: jnp.concatenate([v[:, 64:], v[:, :64]], axis=-1)
    low = jnp.where(lane < 64, a, turn(b))
    high = jnp.where(lane < 64, turn(a), b)
    first = at[3] == 0
    keep_ref[...] = jnp.where(first, low, high)
    send_ref[...] = jnp.where(first, high, low).astype(BF)


def pack(at, own, plus, minus, low, high):
    return pl.pallas_call(
        pack_kernel,
        out_shape=(jax.ShapeDtypeStruct((1024, 128), F32), jax.ShapeDtypeStruct((1024, 128), BF)),
        in_specs=[SMEM] + [VMEM] * 5,
        out_specs=(VMEM, VMEM),
        compiler_params=pltpu.CompilerParams(vmem_limit_bytes=12 << 20),
        name="pack",
    )(at, own, plus, minus, low, high)


def late_kernel(at, rank, s_ref, u_ref, v_ref, out_ref):
    lane = lax.broadcasted_iota(jnp.int32, (1, 128), 1)
    slot = lax.broadcasted_iota(jnp.int32, (256, 1), 0)
    packed = s_ref[...].astype(F32)
    turned = jnp.concatenate([packed[:, 64:], packed[:, :64]], axis=-1)
    s = jnp.concatenate([jnp.where(lane < 64, packed, turned), jnp.where(lane < 64, turned, packed)], axis=0)
    s = s.astype(BF)
    total = []
    for i in range(2):
        back = lax.dot_general(v_ref[i], s, (((0,), (0,)), ((), ())), preferred_element_type=F32)
        keep = jnp.logical_and(slot < rank[2 * (2 * at[0] + at[1]) + i], (lane < 64) == (i == 0))
        back = jnp.where(keep, back, 0.0).astype(BF)
        total.append(jnp.dot(u_ref[i], back, preferred_element_type=F32))
    out_ref[...] = total[0] + total[1]


def late(at, panel_rank, s, u, v):
    return pl.pallas_call(
        late_kernel,
        out_shape=jax.ShapeDtypeStruct((1024, 128), F32),
        in_specs=[SMEM, SMEM, VMEM, VMEM, VMEM],
        out_specs=VMEM,
        compiler_params=pltpu.CompilerParams(vmem_limit_bytes=12 << 20),
        cost_estimate=pl.CostEstimate(flops=4 * 2 * 256 * 1024 * 128, bytes_accessed=3 << 20, transcendentals=0),
        name="late",
    )(at, panel_rank, s, u, v)


def last_kernel(keep_ref, came_ref, late_ref, out_ref):
    v = keep_ref[...] + came_ref[...].astype(F32) - late_ref[...]
    t = v.T.astype(BF)
    out_ref[0] = t[:64]
    out_ref[1] = t[64:]


def last(keep, came, correction):
    return pl.pallas_call(
        last_kernel,
        out_shape=jax.ShapeDtypeStruct((2, 64, 1024), BF),
        in_specs=[VMEM] * 3,
        out_specs=VMEM,
        compiler_params=pltpu.CompilerParams(vmem_limit_bytes=8 << 20),
        name="last",
    )(keep, came, correction)


def panel_kernel(at, *refs):
    held, (u_ref, v_ref, sem) = refs[:8], refs[8:]
    copies = []
    for n, ref in enumerate(held):
        y = lax.rem(at[2] + n % 4, 4)
        co = at[4] if n < 4 else 1 - at[4]
        for m in range(2):
            xl = at[3] if m == 0 else 1 - at[3]
            rows = pl.multiple_of(y * 256 + xl * 128 + co * 64, 64)
            for f, out in enumerate((u_ref, v_ref)):
                copies.append(pltpu.make_async_copy(ref.at[m, f], out.at[:, pl.ds(rows, 64), :], sem))
    for c in copies:
        c.start()
    for c in copies:
        c.wait()


def whole_panel(at, u, v):
    both = jnp.stack([u, v])
    pair = jnp.stack([both, swap(both, "xl")])
    before = move(pair, "y", 1)
    after = move(pair, "y", -1)
    far = move(before, "y", 1)
    held = [pair, after, far, before]
    held += [swap(a, "co") for a in held]
    whole = jax.ShapeDtypeStruct((2, 1024, 256), BF)
    return pl.pallas_call(
        panel_kernel,
        out_shape=(whole, whole),
        in_specs=[SMEM] + [ANY] * 8,
        out_specs=(VMEM, ANY),
        scratch_shapes=[pltpu.SemaphoreType.DMA(())],
        compiler_params=pltpu.CompilerParams(vmem_limit_bytes=4 << 20),
        cost_estimate=pl.CostEstimate(flops=0, bytes_accessed=4 << 20, transcendentals=0),
        name="whole_panel",
    )(at, *held)


def shards(x_rhs, panel_u, panel_v, panel_rank, tile_p, tile_q, tile_rank):
    z, xh, y, xl, co = (lax.axis_index(a) for a in ALL)
    at = jnp.stack([z, xh, y, xl, co]).astype(jnp.int32)

    mine, theirs = split_columns(at, x_rhs)
    came = swap(theirs, "co")
    same = co == xh
    first, second = jnp.where(same, mine, came), jnp.where(same, came, mine)
    own = jnp.stack([first, second, swap(second, "xh")])
    p1, m1 = move(own, "z", 1), move(own, "z", -1)
    p2, m2 = move(p1, "z", 1), move(m1, "z", -1)
    p3, m3 = move(p2, "z", 1), move(m2, "z", -1)
    p4, m4 = move(p3.reshape(6, 64, 512)[:3], "z", 1), move(m3.reshape(6, 64, 512)[3:], "z", -1)
    messages = (own, p1, m1, p2, m2, p3, m3, p4, m4)
    crossed = (
        swap(jnp.stack([own[0], p1[0], m1[0]]), "xh"),
        swap(jnp.stack([p2[0], m2[0]]), "xh"),
        swap(jnp.stack([p3[0], m3[0]]), "xh"),
        swap(p4[None, :2], "xh"),
    )
    qb = swap(tile_q, "co")
    pb = swap(tile_p, "co")
    rank_b = swap(tile_rank, "co")
    u, v = whole_panel(at, panel_u, panel_v)

    early = project_early(at, messages[:7], u)
    row, other = project(at, panel_rank, p4, m4, u, early)
    got = swap(other, "xl")
    row = jnp.where(xl == lax.rem(z, 2), row, got)
    high = y // 2
    got = swap(lax.dynamic_slice_in_dim(row, 2 - 2 * high, 2, 0), "y", 2)
    two = jnp.where(y == z // 2, lax.dynamic_slice_in_dim(row, 2 * high, 2, 0), got)
    low = lax.rem(y, 2)
    got = swap(lax.dynamic_index_in_dim(two, 1 - low, 0, False), "y", 1)
    s = sweep_part(at, lax.dynamic_index_in_dim(two, low, 0, False), got, v)
    s = s + swap(s, "xh")
    right = move(s, "z", -1)
    pair = s + right
    near = pair + move(s, "z", 1)
    s = near + move(near, "z", -3) + move(pair, "z", 3)

    tiles = (tile_q, qb, tile_p, pb)
    operands = (*messages, *crossed, *tiles)
    plus, minus, own_sum, after = base(0, at, tile_rank, rank_b, *operands)
    plus, minus, own_sum, before = base(1, at, tile_rank, rank_b, *operands, plus, minus, own_sum)
    plus, minus = move(plus, "y", 1), move(minus, "y", -1)
    up = move(after + plus[0], "y", 1)
    down = move(before + minus[0], "y", -1)
    keep, away = pack(at, own_sum, plus, minus, up, down)
    came = swap(away, "xl")
    correction = late(at, panel_rank, s, u, v)
    out = last(keep, came, correction)
    return out.swapaxes(1, 2)


def solution(mesh):
    finer = Mesh(mesh.devices.reshape(8, 2, 4, 2, 2), ALL)
    return jax.shard_map(
        shards,
        mesh=finer,
        in_specs=(
            P(COL, ROW, None),
            P(ROW, COL, None),
            P(ROW, COL, None),
            P(),
            P(ROW, COL, None, None),
            P(ROW, COL, None, None),
            P(ROW, COL),
        ),
        out_specs=P(ROW, None, COL),
        check_vma=False,
    )
```
